512 devices in a mesh: blk: 32 (over z_lo, y, core), rows: 16 (over x, z_hi).
Axes of the slice: x: 4, y: 8, z: 8 (z_hi: 4, z_lo: 2; z = z_hi * 2 + z_lo), core: 2. Of those that a mesh axis runs over, the one named last changes fastest.
Arguments:
- covariance: float32 [16384, 2, 32, 256], P('rows', None, 'blk'), may hold values from 0 to 5, as said below
- panel_order: int32 [64], replicated, may hold values from 0 to 63, each once
Outputs:
- factored: float32 [16384, 2, 32, 256], P('rows', None, 'blk')
The draws below stay inside these ranges and needn't reach their ends.
Inputs may be any that keep to these rules, and one draw needn't show every extreme that they name: covariance is symmetric and positive definite. `panel_order`: every panel appears once; panel j is held by index j % 32 of blk.
All inputs are finite; a program needn't handle non-finite values.
Results may differ from the reference program's by a relative error of at most 0.0003.
Values sent between devices are 32-bit elements; how exact they have to be, the bound alone decides.
No kernel may reach another device: no remote copies, remote signals or barrier semaphores. Data moves between devices by JAX's collectives and lax.ppermute only.
A program may use at most 64 MiB of HBM per device.

```python
import jax
import jax.numpy as jnp
from jax import lax

ORDER = 16384
PANEL = 256
SECTIONS = 2
PANELS = 64
OWNERS = 32
PAN_DEV = 2


def draw_covariance(key, part):
    base_key = jax.random.fold_in(key, 11)
    point_key = jax.random.fold_in(base_key, 0)
    points = jax.random.uniform(point_key, (ORDER, 3), jnp.float32)
    squared = jnp.zeros((ORDER, ORDER), jnp.float32)
    for axis_index in range(3):
        column = points[:, axis_index]
        spread_gap = column[:, None] - column[None, :]
        squared = squared + spread_gap * spread_gap
    distance = jnp.sqrt(squared)
    kernel = jnp.exp(-distance / 0.2)
    indices = jnp.arange(ORDER)
    kernel = jnp.where(indices[:, None] == indices[None, :], kernel + 0.25, kernel)
    return kernel.reshape(ORDER, PAN_DEV, OWNERS, PANEL)


def setup_inputs(seed: int = 0) -> dict:
    seeds = jax.random.split(jax.random.key(seed), 3)
    covariance = draw_covariance(jax.random.fold_in(seeds[2], 71), 0)
    panel_order = jax.random.permutation(seeds[1], PANELS).astype(jnp.int32)
    return dict(covariance=covariance, panel_order=panel_order)


def inverse_factor(diagonal_block):
    lower_factor = jnp.linalg.cholesky(diagonal_block)
    identity_block = jnp.eye(diagonal_block.shape[0], dtype=diagonal_block.dtype)
    return lax.linalg.triangular_solve(lower_factor, identity_block, left_side=True, lower=True)

def reference(covariance, panel_order):
    matrix_order = covariance.shape[0]
    panel_width = covariance.shape[3]
    panel_total = matrix_order // panel_width
    working = covariance.reshape(matrix_order, matrix_order)
    frozen = jnp.zeros((panel_total,), jnp.float32)
    for round_index in range(SECTIONS):
        target = panel_order[round_index]
        first_column = (target * panel_width).astype(jnp.int32)
        column_panel = lax.dynamic_slice_in_dim(working, first_column, panel_width, 1)
        diagonal_block = lax.dynamic_slice_in_dim(column_panel, first_column, panel_width, 0)
        inverse = inverse_factor(diagonal_block)
        factor = jnp.dot(column_panel.astype(jnp.float32), inverse.T.astype(jnp.float32), precision=lax.Precision.HIGHEST, preferred_element_type=jnp.float32)
        frozen = frozen + (jnp.arange(panel_total) == target).astype(jnp.float32)
        live_rows = jnp.repeat(1.0 - frozen, panel_width)
        masked_factor = factor * live_rows[:, None]
        working = working - jnp.dot(factor.astype(jnp.float32), masked_factor.T.astype(jnp.float32), precision=lax.Precision.HIGHEST, preferred_element_type=jnp.float32)
        working = lax.dynamic_update_slice_in_dim(working, factor, first_column, 1)
    return working.reshape(covariance.shape)
```

```python
import jax
import jax.numpy as jnp
from jax import lax
from jax.experimental import pallas as pl
from jax.experimental.pallas import tpu as pltpu
from jax.sharding import Mesh, PartitionSpec as P

HI = lax.Precision.HIGHEST
LEAF = 128
PIV = 8


def mm(a, b, ca=1, cb=0, precision=HI):
    return lax.dot_general(
        a, b, (((ca,), (cb,)), ((), ())), precision=precision, preferred_element_type=jnp.float32
    )


def leaf_inverse_factor(matrix):
    tiles = LEAF // 8
    shape = (8, LEAF)
    sub = lax.broadcasted_iota(jnp.int32, shape, 0)
    lane = lax.broadcasted_iota(jnp.int32, shape, 1)
    s = [matrix[8 * t : 8 * t + 8, :] for t in range(tiles)]
    v = [jnp.where(sub + 8 * t == lane, 1.0, 0.0).astype(jnp.float32) for t in range(tiles)]
    scale = [None] * tiles
    for k in range(0, LEAF, PIV):
        t, base = k // 8, k % 8
        piv = {}
        for a in range(PIV):
            for c in range(a + 1):
                piv[a, c] = jnp.broadcast_to(s[t][base + a : base + a + 1, k + c : k + c + 1], shape)
        rd, low = [], {}
        for j in range(PIV):
            rd.append(1.0 / piv[j, j])
            for i in range(j + 1, PIV):
                low[i, j] = piv[i, j] * rd[j]
            for i in range(j + 1, PIV):
                for m in range(j + 1, i + 1):
                    piv[i, m] = piv[i, m] - low[i, j] * piv[m, j]
            root = lax.rsqrt(piv[j, j])
            scale[t] = root if base + j == 0 else jnp.where(sub == base + j, root, scale[t])
        rows_s, rows_v = [], []
        for u in range(t, tiles):
            raw, coef = [], []
            for j in range(PIV):
                c = jnp.broadcast_to(s[u][:, k + j : k + j + 1], shape)
                for m in range(j):
                    c = c - raw[m] * low[j, m]
                raw.append(c)
                c = c * rd[j]
                coef.append(jnp.where(sub > base + j, c, 0.0) if u == t else c)
            for j in range(PIV):
                if u == t:
                    rows_s.append(jnp.broadcast_to(s[t][base + j : base + j + 1, :], shape))
                    rows_v.append(jnp.broadcast_to(v[t][base + j : base + j + 1, :], shape))
                s[u] = s[u] - coef[j] * rows_s[j]
                v[u] = v[u] - coef[j] * rows_v[j]
    return jnp.concatenate([v[t] * scale[t] for t in range(tiles)], axis=0)


def factor_kernel(core_ref, own_ref, other_ref, g_ref, m_ref, h_ref, l_ref):
    n = g_ref.shape[0]
    half = n // 2
    core = core_ref[0]
    for source, part in ((own_ref, core), (other_ref, 1 - core)):
        for c in range(16):
            row = pl.multiple_of(c * 16 + part * 8, 8)
            for i, (top, left) in enumerate(((0, 0), (half, 0), (half, half))):
                for ch in range(2):
                    m_ref[pl.ds(row + top, 8), left + ch * 128 : left + ch * 128 + 128] = source[
                        c % 4, c // 4, i, pl.ds(ch, 8, stride=2), :
                    ]
    h_ref[...] = jnp.zeros_like(h_ref)
    g_ref[...] = jnp.zeros_like(g_ref)
    count = n // LEAF

    def step(k, carry):
        at = pl.multiple_of(k * LEAF, LEAF)
        own = leaf_inverse_factor(m_ref[pl.ds(at, LEAF), pl.ds(at, LEAF)])
        g_ref[pl.ds(at, LEAF), pl.ds(at, LEAF)] = own
        for kk in range(count):

            @pl.when(k == kk)
            def _():
                lo, hi = kk * LEAF, (kk + 1) * LEAF
                if kk:
                    g_ref[lo:hi, 0:lo] = mm(own, h_ref[lo:hi, 0:lo])
                if kk + 1 < count:
                    low = mm(m_ref[hi:n, lo:hi], own, 1, 1)
                    l_ref[hi:n, :] = low
                    for j in range(kk + 1, count):
                        a, b = j * LEAF, (j + 1) * LEAF
                        m_ref[a:n, a:b] = m_ref[a:n, a:b] - mm(l_ref[a:n, :], l_ref[a:b, :], 1, 1)
                    h_ref[hi:n, 0:hi] = h_ref[hi:n, 0:hi] - mm(l_ref[hi:n, :], g_ref[lo:hi, 0:hi])

        return carry

    lax.fori_loop(0, count, step, 0)


def inverse_factor(core, own, other):
    n = 512
    whole = pl.BlockSpec(memory_space=pltpu.VMEM)
    return pl.pallas_call(
        factor_kernel,
        out_shape=jax.ShapeDtypeStruct((n, n), jnp.float32),
        in_specs=[pl.BlockSpec(memory_space=pltpu.SMEM), whole, whole],
        out_specs=whole,
        scratch_shapes=[
            pltpu.VMEM((n, n), jnp.float32),
            pltpu.VMEM((n, n), jnp.float32),
            pltpu.VMEM((n, LEAF), jnp.float32),
        ],
        cost_estimate=pl.CostEstimate(flops=2 * 8 * n**3, bytes_accessed=8 * n * n, transcendentals=n),
    )(core, own, other)


def update_kernel(info_ref, w_ref, own_ref, other_ref, y_ref, g_ref, o_ref, u_ref, z_ref):
    n = g_ref.shape[0]
    step = pl.program_id(0)

    @pl.when(step == 0)
    def _():
        for j in range(4):
            for c in range(16):
                for s in range(2):
                    z_ref[s * 256 + c * 16 : s * 256 + c * 16 + 16, j * 128 : j * 128 + 128] = y_ref[
                        c % 4, c // 4, s, pl.ds(j, 16, stride=4), :
                    ]
        u_ref[...] = mm(g_ref[...], z_ref[...])
        for slot in range(2):
            for s in range(2):

                @pl.when(info_ref[1 + slot] == s)
                def _():
                    rows = lax.broadcasted_iota(jnp.int32, (n, 256), 0)
                    cols = lax.broadcasted_iota(jnp.int32, (n, 256), 1)
                    u_ref[:, slot * 256 : slot * 256 + 256] = jnp.where(
                        rows == cols + s * 256, 1.0, 0.0
                    ).astype(jnp.float32)

        solved = mm(g_ref[...], u_ref[...], 0, 0)
        at = 0
        for yh in range(4):
            for zlo in range(2):
                for half in range(2):
                    for s in range(2):
                        row = s * 256 + (half * 8 + zlo * 4 + yh) * 16
                        z_ref[at : at + 16, :] = solved[row : row + 16, :]
                        at += 16

    def rows_of(source, yl):
        for ch in range(2):
            panel = jnp.concatenate(
                [source[yh, yl, pl.ds(ch, 128, stride=2), :] for yh in range(4)], axis=0
            )
            change = mm(panel, z_ref[...], 0, 0)
            for j in range(4):
                hit = info_ref[1 + j // 2] >= 0
                keep = jnp.where(hit, 0.0, 1.0).astype(jnp.float32)
                sign = jnp.where(hit, 1.0, -1.0).astype(jnp.float32)
                at = pl.ds(ch * 512 + j, 128, stride=4)
                o_ref[at, :] = keep * w_ref[at, :] + sign * change[:, j * 128 : j * 128 + 128]

    for o, source in enumerate((own_ref, other_ref)):
        for yl in range(2):

            @pl.when(step == o * 2 + yl)
            def _():
                rows_of(source, yl)


def update(info, working, own, other, across, factor):
    n = 512
    whole = pl.BlockSpec(memory_space=pltpu.VMEM)

    def block(step, info_ref):
        core = info_ref[0]
        part = jnp.where(step >= 2, 1 - core, core)
        return (step % 2) * 2 + part, 0

    return pl.pallas_call(
        update_kernel,
        out_shape=jax.ShapeDtypeStruct(working.shape, jnp.float32),
        grid_spec=pltpu.PrefetchScalarGridSpec(
            num_scalar_prefetch=1,
            grid=(4,),
            in_specs=[pl.BlockSpec((1024, 128), block), whole, whole, whole, whole],
            out_specs=pl.BlockSpec((1024, 128), block),
            scratch_shapes=[pltpu.VMEM((n, n), jnp.float32), pltpu.VMEM((n, n), jnp.float32)],
        ),
        cost_estimate=pl.CostEstimate(flops=8 * n**3, bytes_accessed=8 * 2**20, transcendentals=0),
    )(info, working, own, other, across, factor)


def swap(array, axis):
    return lax.ppermute(array, axis, [(0, 1), (1, 0)])


def ordered_pair(own, other, index):
    first = jnp.where(index == 0, own, other)
    second = jnp.where(index == 0, other, own)
    return jnp.stack([first, second])


def spread_pairs(swapped):
    pairs = []
    for source in range(512):
        blk, row = divmod(source, 16)
        upper = (row >= 8) != swapped
        target_row = blk // 4 + (8 if upper else 0)
        target_blk = (row % 8) * 4 + blk % 4
        pairs.append((source, target_blk * 16 + target_row))
    return pairs


EVERY = ("zlo", "y", "core", "x", "zhi")
ROWS = ("x", "zhi")


def pick(array, axis, index):
    return lax.dynamic_index_in_dim(array, index, axis, keepdims=False)


def exchange(array, axis):
    return lax.all_to_all(array, axis, 0, 0, tiled=True)


def copies(array, count):
    return jnp.broadcast_to(array, (count, *array.shape))


def doubled(array, axis):
    index = lax.axis_index(axis)
    near = lax.ppermute(array, axis, [(i, i ^ 1) for i in range(4)])
    pair = ordered_pair(array, near, index % 2)
    far = lax.ppermute(pair, axis, [(i, i ^ 2) for i in range(4)])
    return ordered_pair(pair, far, index // 2).reshape(4, *array.shape)


def local(covariance, panel_order):
    row = lax.axis_index(ROWS)
    core = lax.axis_index("core")
    zlo = lax.axis_index("zlo")
    blk = lax.axis_index(("zlo", "y", "core"))
    working = covariance.reshape(4096, 128)
    target = [panel_order[0], panel_order[1]]
    root = [q // 4 for q in target]
    owner = [q % 32 for q in target]
    slot = [q // 32 for q in target]

    cand = [lax.dynamic_slice_in_dim(working, (q % 4) * 1024, 1024, 0).reshape(4, 4, 64, 128) for q in target]
    got = exchange(jnp.stack(cand, axis=2), "x")
    got = jnp.stack([pick(got[:, :, s], 0, root[s] // 4) for s in range(2)], axis=1)
    got = exchange(got, "zhi")
    chunk = jnp.stack([pick(got[:, s], 0, root[s] % 4) for s in range(2)])
    by_slot = chunk.reshape(2, 16, 2, 2, 128)

    part = [pick(by_slot[1 if i else 0], 1, slot[1 if i == 2 else 0]) for i in range(3)]
    blocks = jnp.stack(part).reshape(3, 2, 16, 128)
    source = jnp.stack([owner[0], owner[0], owner[1]])
    other = swap(pick(blocks, 1, 1 - core), "core")
    mine = jnp.where((source % 2 == core)[:, None, None], pick(blocks, 1, core), other)
    mine = jnp.where((source // 16 == zlo)[:, None, None], mine, swap(mine, "zlo"))
    spread = exchange(copies(mine, 8), "y")
    from_y = source // 2 % 8
    mine = jnp.stack([pick(spread[:, i], 0, from_y[i]) for i in range(3)])
    ready = mine
    mine = doubled(doubled(mine, "x"), "zhi")
    factor = inverse_factor(core.reshape(1), mine, swap(mine, "core"))

    low, high = by_slot[:, :, 0].reshape(64, 128), by_slot[:, :, 1].reshape(64, 128)
    upper = row >= 8
    piece_a = lax.ppermute(jnp.where(upper, high, low), EVERY, spread_pairs(False))
    piece_b = lax.ppermute(jnp.where(upper, low, high), EVERY, spread_pairs(True))
    pieces = jnp.stack([jnp.where(upper, piece_b, piece_a), jnp.where(upper, piece_a, piece_b)])
    pieces = ordered_pair(pieces, swap(pieces, "zlo"), zlo).reshape(256, 128)
    pieces = lax.optimization_barrier((pieces, ready))[0]
    pieces = exchange(copies(pieces, 8), "y").reshape(4, 2, 256, 128)

    across = lax.optimization_barrier((doubled(chunk, "x"), pieces))[0]
    across = exchange(copies(across, 4), "zhi")

    hits = [jnp.int32(-1), jnp.int32(-1)]
    for i in range(2):
        for s in range(2):
            hits[i] = jnp.where(target[s] == i * 32 + blk, s, hits[i])
    info = jnp.stack([core, hits[0], hits[1]]).astype(jnp.int32)
    result = update(info, working, pieces, swap(pieces, "core"), across, factor)
    return result.reshape(1024, 2, 1, 256)


def solution(mesh):
    fine = Mesh(mesh.devices.reshape(2, 8, 2, 4, 4), EVERY)
    spec = P(ROWS, None, ("zlo", "y", "core"), None)
    return jax.shard_map(local, mesh=fine, in_specs=(spec, P()), out_specs=spec, check_vma=False)
```

```python
import jax
import jax.numpy as jnp
from jax import lax
from jax.experimental import pallas as pl
from jax.experimental.pallas import tpu as pltpu
from jax.sharding import Mesh, PartitionSpec as P


HI = lax.Precision.HIGHEST
LEAF = 128
PIV = 8


def mm(a, b, ca=1, cb=0, precision=HI):
    return lax.dot_general(
        a, b, (((ca,), (cb,)), ((), ())), precision=precision, preferred_element_type=jnp.float32
    )


def leaf_inverse_factor(matrix):
    tiles = LEAF // 8
    shape = (8, LEAF)
    sub = lax.broadcasted_iota(jnp.int32, shape, 0)
    lane = lax.broadcasted_iota(jnp.int32, shape, 1)
    s = [matrix[8 * t : 8 * t + 8, :] for t in range(tiles)]
    v = [jnp.where(sub + 8 * t == lane, 1.0, 0.0).astype(jnp.float32) for t in range(tiles)]
    scale = [None] * tiles
    for k in range(0, LEAF, PIV):
        t, base = k // 8, k % 8
        piv = {}
        for a in range(PIV):
            for c in range(a + 1):
                piv[a, c] = jnp.broadcast_to(s[t][base + a : base + a + 1, k + c : k + c + 1], shape)
        rd, low = [], {}
        for j in range(PIV):
            rd.append(1.0 / piv[j, j])
            for i in range(j + 1, PIV):
                low[i, j] = piv[i, j] * rd[j]
            for i in range(j + 1, PIV):
                for m in range(j + 1, i + 1):
                    piv[i, m] = piv[i, m] - low[i, j] * piv[m, j]
            root = lax.rsqrt(piv[j, j])
            scale[t] = root if base + j == 0 else jnp.where(sub == base + j, root, scale[t])
        rows_s, rows_v = [], []
        for u in range(t, tiles):
            raw, coef = [], []
            for j in range(PIV):
                c = jnp.broadcast_to(s[u][:, k + j : k + j + 1], shape)
                for m in range(j):
                    c = c - raw[m] * low[j, m]
                raw.append(c)
                c = c * rd[j]
                coef.append(jnp.where(sub > base + j, c, 0.0) if u == t else c)
            for j in range(PIV):
                if u == t:
                    rows_s.append(jnp.broadcast_to(s[t][base + j : base + j + 1, :], shape))
                    rows_v.append(jnp.broadcast_to(v[t][base + j : base + j + 1, :], shape))
                s[u] = s[u] - coef[j] * rows_s[j]
                v[u] = v[u] - coef[j] * rows_v[j]
    return jnp.concatenate([v[t] * scale[t] for t in range(tiles)], axis=0)


def factor_kernel(core_ref, own_ref, other_ref, g_ref, m_ref, h_ref, l_ref):
    n = g_ref.shape[0]
    half = n // 2
    core = core_ref[0]
    for source, part in ((own_ref, core), (other_ref, 1 - core)):
        for c in range(16):
            row = pl.multiple_of(c * 16 + part * 8, 8)
            for i, (top, left) in enumerate(((0, 0), (half, 0), (half, half))):
                for ch in range(2):
                    m_ref[pl.ds(row + top, 8), left + ch * 128 : left + ch * 128 + 128] = source[
                        c // 4, c % 4, i, pl.ds(ch, 8, stride=2), :
                    ]
    h_ref[...] = jnp.zeros_like(h_ref)
    g_ref[...] = jnp.zeros_like(g_ref)
    count = n // LEAF

    def step(k, carry):
        at = pl.multiple_of(k * LEAF, LEAF)
        own = leaf_inverse_factor(m_ref[pl.ds(at, LEAF), pl.ds(at, LEAF)])
        g_ref[pl.ds(at, LEAF), pl.ds(at, LEAF)] = own
        for kk in range(count):

            @pl.when(k == kk)
            def _():
                lo, hi = kk * LEAF, (kk + 1) * LEAF
                if kk:
                    g_ref[lo:hi, 0:lo] = mm(own, h_ref[lo:hi, 0:lo])
                if kk + 1 < count:
                    low = mm(m_ref[hi:n, lo:hi], own, 1, 1)
                    l_ref[hi:n, :] = low
                    for j in range(kk + 1, count):
                        a, b = j * LEAF, (j + 1) * LEAF
                        m_ref[a:n, a:b] = m_ref[a:n, a:b] - mm(l_ref[a:n, :], l_ref[a:b, :], 1, 1)
                    h_ref[hi:n, 0:hi] = h_ref[hi:n, 0:hi] - mm(l_ref[hi:n, :], g_ref[lo:hi, 0:hi])

        return carry

    lax.fori_loop(0, count, step, 0)


def inverse_factor(core, own, other):
    n = 512
    whole = pl.BlockSpec(memory_space=pltpu.VMEM)
    return pl.pallas_call(
        factor_kernel,
        out_shape=jax.ShapeDtypeStruct((n, n), jnp.float32),
        in_specs=[pl.BlockSpec(memory_space=pltpu.SMEM), whole, whole],
        out_specs=whole,
        scratch_shapes=[
            pltpu.VMEM((n, n), jnp.float32),
            pltpu.VMEM((n, n), jnp.float32),
            pltpu.VMEM((n, LEAF), jnp.float32),
        ],
        cost_estimate=pl.CostEstimate(flops=2 * 8 * n**3, bytes_accessed=8 * n * n, transcendentals=n),
    )(core, own, other)


def update_kernel(info_ref, w_ref, own_ref, other_ref, y_ref, g_ref, o_ref, u_ref, z_ref):
    n = g_ref.shape[0]
    step = pl.program_id(0)

    @pl.when(step == 0)
    def _():
        for j in range(4):
            for c in range(16):
                for s in range(2):
                    z_ref[s * 256 + c * 16 : s * 256 + c * 16 + 16, j * 128 : j * 128 + 128] = y_ref[
                        c // 4, c % 4, s, pl.ds(j, 16, stride=4), :
                    ]
        u_ref[...] = mm(g_ref[...], z_ref[...])
        for slot in range(2):
            for s in range(2):

                @pl.when(info_ref[1 + slot] == s)
                def _():
                    rows = lax.broadcasted_iota(jnp.int32, (n, 256), 0)
                    cols = lax.broadcasted_iota(jnp.int32, (n, 256), 1)
                    u_ref[:, slot * 256 : slot * 256 + 256] = jnp.where(
                        rows == cols + s * 256, 1.0, 0.0
                    ).astype(jnp.float32)

        solved = mm(g_ref[...], u_ref[...], 0, 0)
        at = 0
        for yh in range(4):
            for zlo in range(2):
                for half in range(2):
                    for s in range(2):
                        row = s * 256 + (half * 8 + zlo * 4 + yh) * 16
                        z_ref[at : at + 16, :] = solved[row : row + 16, :]
                        at += 16

    def rows_of(source, yl):
        for ch in range(2):
            panel = jnp.concatenate(
                [source[yh, yl, pl.ds(ch, 128, stride=2), :] for yh in range(4)], axis=0
            )
            change = mm(panel, z_ref[...], 0, 0)
            for j in range(4):
                hit = info_ref[1 + j // 2] >= 0
                keep = jnp.where(hit, 0.0, 1.0).astype(jnp.float32)
                sign = jnp.where(hit, 1.0, -1.0).astype(jnp.float32)
                at = pl.ds(ch * 512 + j, 128, stride=4)
                o_ref[at, :] = keep * w_ref[at, :] + sign * change[:, j * 128 : j * 128 + 128]

    for o, source in enumerate((own_ref, other_ref)):
        for yl in range(2):

            @pl.when(step == o * 2 + yl)
            def _():
                rows_of(source, yl)


def update(info, working, own, other, across, factor):
    n = 512
    whole = pl.BlockSpec(memory_space=pltpu.VMEM)

    def block(step, info_ref):
        core = info_ref[0]
        part = jnp.where(step >= 2, 1 - core, core)
        return (step % 2) * 2 + part, 0

    return pl.pallas_call(
        update_kernel,
        out_shape=jax.ShapeDtypeStruct(working.shape, jnp.float32),
        grid_spec=pltpu.PrefetchScalarGridSpec(
            num_scalar_prefetch=1,
            grid=(4,),
            in_specs=[pl.BlockSpec((1024, 128), block), whole, whole, whole, whole],
            out_specs=pl.BlockSpec((1024, 128), block),
            scratch_shapes=[pltpu.VMEM((n, n), jnp.float32), pltpu.VMEM((n, n), jnp.float32)],
        ),
        cost_estimate=pl.CostEstimate(flops=8 * n**3, bytes_accessed=8 * 2**20, transcendentals=0),
    )(info, working, own, other, across, factor)


def swap(array, axis):
    return lax.ppermute(array, axis, [(0, 1), (1, 0)])


def ordered_pair(own, other, index):
    first = jnp.where(index == 0, own, other)
    second = jnp.where(index == 0, other, own)
    return jnp.stack([first, second])


def spread_pairs(swapped):
    pairs = []
    for source in range(512):
        blk, row = divmod(source, 16)
        upper = (row >= 8) != swapped
        target_row = blk // 4 + (8 if upper else 0)
        target_blk = (row % 8) * 4 + blk % 4
        pairs.append((source, target_blk * 16 + target_row))
    return pairs


EVERY = ("zlo", "y", "core", "x", "zhi")
ROWS = ("x", "zhi")


def pick(array, axis, index):
    return lax.dynamic_index_in_dim(array, index, axis, keepdims=False)


def exchange(array, axis):
    return lax.all_to_all(array, axis, 0, 0, tiled=True)


def copies(array, count):
    return jnp.broadcast_to(array, (count, *array.shape))


def doubled(array, axis):
    index = lax.axis_index(axis)
    near = lax.ppermute(array, axis, [(i, i ^ 1) for i in range(4)])
    pair = ordered_pair(array, near, index % 2)
    far = lax.ppermute(pair, axis, [(i, i ^ 2) for i in range(4)])
    return ordered_pair(pair, far, index // 2).reshape(4, *array.shape)


def after(array, *others):
    return lax.optimization_barrier((array, *others))[0]


def sections(covariance, panel_order):
    place = lax.axis_index(EVERY)
    row, core, zlo, blk = place & 15, (place >> 4) & 1, place >> 8, place >> 4
    working = covariance.reshape(4096, 128)
    target = [panel_order[0], panel_order[1]]
    root = [q >> 2 for q in target]

    cand = [lax.dynamic_slice_in_dim(working, (q & 3) << 10, 1024, 0).reshape(4, 4, 64, 128) for q in target]
    got = exchange(jnp.stack(cand, axis=2), "x")
    got = jnp.stack([pick(got[:, :, s], 0, root[s] >> 2) for s in range(2)], axis=1)
    got = exchange(got, "zhi")
    chunk = jnp.stack([pick(got[:, s], 0, root[s] & 3) for s in range(2)])
    by_slot = chunk.reshape(2, 16, 2, 2, 128)

    part = [pick(by_slot[1 if i else 0], 1, target[1 if i == 2 else 0] >> 5) for i in range(3)]
    blocks = jnp.stack(part).reshape(3, 2, 16, 128)
    source = [target[0], target[0], target[1]]

    def chosen(shift, index, own, other):
        return jnp.stack([jnp.where(((source[i] >> shift) & 1) == index, own[i], other[i]) for i in range(3)])

    other = swap(pick(blocks, 1, 1 - core), "core")
    mine = chosen(0, core, pick(blocks, 1, core), other)
    other = swap(mine, "zlo")
    placed = mine = chosen(4, zlo, mine, other)
    spread = exchange(copies(mine, 8), "y")
    mine = jnp.stack([pick(spread[:, i], 0, (source[i] >> 1) & 7) for i in range(3)])
    ready = mine
    mine = exchange(copies(mine, 4), "zhi")
    mine = exchange(copies(mine, 4), "x")
    other = swap(mine, "core")
    factor = inverse_factor(core.reshape(1), mine, other)

    low, high = by_slot[:, :, 0].reshape(64, 128), by_slot[:, :, 1].reshape(64, 128)
    upper = row >= 8
    send_a = after(jnp.where(upper, high, low), placed)
    send_b = after(jnp.where(upper, low, high), placed)
    piece_a = lax.ppermute(send_a, EVERY, spread_pairs(False))
    piece_b = lax.ppermute(send_b, EVERY, spread_pairs(True))
    pieces = jnp.stack([jnp.where(upper, piece_b, piece_a), jnp.where(upper, piece_a, piece_b)])
    pieces = after(pieces, ready)
    other = swap(pieces, "zlo")
    pieces = ordered_pair(pieces, other, zlo).reshape(256, 128)
    pieces = after(pieces, mine)
    pieces = exchange(copies(pieces, 8), "y").reshape(4, 2, 256, 128)
    other = swap(pieces, "core")

    across = doubled(after(chunk, ready), "zhi")
    across = after(across, pieces)
    across = exchange(copies(across, 4), "x")

    hits = [jnp.int32(-1), jnp.int32(-1)]
    for i in range(2):
        for s in range(2):
            hits[i] = jnp.where(target[s] == i * 32 + blk, s, hits[i])
    info = jnp.stack([core, hits[0], hits[1]]).astype(jnp.int32)
    result = update(info, working, pieces, other, across, factor)
    return result.reshape(1024, 2, 1, 256)


def solution(mesh):
    fine = Mesh(mesh.devices.reshape(2, 8, 2, 4, 4), EVERY)
    spec = P(ROWS, None, ("zlo", "y", "core"), None)
    return jax.shard_map(sections, mesh=fine, in_specs=(spec, P()), out_specs=spec, check_vma=False)
```

```python
import jax
import jax.numpy as jnp
from jax import lax
from jax.experimental import pallas as pl
from jax.experimental.pallas import tpu as pltpu
from jax.sharding import Mesh, PartitionSpec as P


HI = lax.Precision.HIGHEST
LEAF = 128
PIV = 8


def mm(a, b, ca=1, cb=0, precision=HI):
    return lax.dot_general(
        a, b, (((ca,), (cb,)), ((), ())), precision=precision, preferred_element_type=jnp.float32
    )


def leaf_inverse_factor(matrix):
    tiles = LEAF // 8
    shape = (8, LEAF)
    sub = lax.broadcasted_iota(jnp.int32, shape, 0)
    lane = lax.broadcasted_iota(jnp.int32, shape, 1)
    s = [matrix[8 * t : 8 * t + 8, :] for t in range(tiles)]
    v = [jnp.where(sub + 8 * t == lane, 1.0, 0.0).astype(jnp.float32) for t in range(tiles)]
    scale = [None] * tiles
    for k in range(0, LEAF, PIV):
        t, base = k // 8, k % 8
        piv = {}
        for a in range(PIV):
            for c in range(a + 1):
                piv[a, c] = jnp.broadcast_to(s[t][base + a : base + a + 1, k + c : k + c + 1], shape)
        rd, low = [], {}
        for j in range(PIV):
            rd.append(1.0 / piv[j, j])
            for i in range(j + 1, PIV):
                low[i, j] = piv[i, j] * rd[j]
            for i in range(j + 1, PIV):
                for m in range(j + 1, i + 1):
                    piv[i, m] = piv[i, m] - low[i, j] * piv[m, j]
            root = lax.rsqrt(piv[j, j])
            scale[t] = root if base + j == 0 else jnp.where(sub == base + j, root, scale[t])
        rows_s, rows_v = [], []
        for u in range(t, tiles):
            raw, coef = [], []
            for j in range(PIV):
                c = jnp.broadcast_to(s[u][:, k + j : k + j + 1], shape)
                for m in range(j):
                    c = c - raw[m] * low[j, m]
                raw.append(c)
                c = c * rd[j]
                coef.append(jnp.where(sub > base + j, c, 0.0) if u == t else c)
            for j in range(PIV):
                if u == t:
                    rows_s.append(jnp.broadcast_to(s[t][base + j : base + j + 1, :], shape))
                    rows_v.append(jnp.broadcast_to(v[t][base + j : base + j + 1, :], shape))
                s[u] = s[u] - coef[j] * rows_s[j]
                v[u] = v[u] - coef[j] * rows_v[j]
    return jnp.concatenate([v[t] * scale[t] for t in range(tiles)], axis=0)


def factor_kernel(core_ref, own_ref, other_ref, g_ref, m_ref, h_ref, l_ref):
    n = g_ref.shape[0]
    half = n // 2
    core = core_ref[0]
    for source, part in ((own_ref, core), (other_ref, 1 - core)):
        for c in range(16):
            row = pl.multiple_of(c * 16 + part * 8, 8)
            for i, (top, left) in enumerate(((0, 0), (half, 0), (half, half))):
                for ch in range(2):
                    m_ref[pl.ds(row + top, 8), left + ch * 128 : left + ch * 128 + 128] = source[
                        c // 4, c % 4, i, pl.ds(ch, 8, stride=2), :
                    ]
    h_ref[...] = jnp.zeros_like(h_ref)
    g_ref[...] = jnp.zeros_like(g_ref)
    count = n // LEAF

    def step(k, carry):
        at = pl.multiple_of(k * LEAF, LEAF)
        own = leaf_inverse_factor(m_ref[pl.ds(at, LEAF), pl.ds(at, LEAF)])
        g_ref[pl.ds(at, LEAF), pl.ds(at, LEAF)] = own
        for kk in range(count):

            @pl.when(k == kk)
            def _():
                lo, hi = kk * LEAF, (kk + 1) * LEAF
                if kk:
                    g_ref[lo:hi, 0:lo] = mm(own, h_ref[lo:hi, 0:lo])
                if kk + 1 < count:
                    low = mm(m_ref[hi:n, lo:hi], own, 1, 1)
                    l_ref[hi:n, :] = low
                    for j in range(kk + 1, count):
                        a, b = j * LEAF, (j + 1) * LEAF
                        m_ref[a:n, a:b] = m_ref[a:n, a:b] - mm(l_ref[a:n, :], l_ref[a:b, :], 1, 1)
                    h_ref[hi:n, 0:hi] = h_ref[hi:n, 0:hi] - mm(l_ref[hi:n, :], g_ref[lo:hi, 0:hi])

        return carry

    lax.fori_loop(0, count, step, 0)


def inverse_factor(core, own, other):
    n = 512
    whole = pl.BlockSpec(memory_space=pltpu.VMEM)
    return pl.pallas_call(
        factor_kernel,
        out_shape=jax.ShapeDtypeStruct((n, n), jnp.float32),
        in_specs=[pl.BlockSpec(memory_space=pltpu.SMEM), whole, whole],
        out_specs=whole,
        scratch_shapes=[
            pltpu.VMEM((n, n), jnp.float32),
            pltpu.VMEM((n, n), jnp.float32),
            pltpu.VMEM((n, LEAF), jnp.float32),
        ],
        cost_estimate=pl.CostEstimate(flops=2 * 8 * n**3, bytes_accessed=8 * n * n, transcendentals=n),
    )(core, own, other)


def solve_kernel(info_ref, y0_ref, y1_ref, y2_ref, y3_ref, g_ref, o_ref, y_ref, u_ref):
    n = g_ref.shape[0]
    for shift, source in enumerate((y0_ref, y1_ref, y2_ref, y3_ref)):
        x = lax.rem(info_ref[3] + 4 - shift, 4)
        for zhi in range(4):
            for s in range(2):
                row = pl.multiple_of(s * 256 + x * 64 + zhi * 16, 16)
                for j in range(4):
                    y_ref[pl.ds(row, 16), j * 128 : j * 128 + 128] = source[zhi, s, pl.ds(j, 16, stride=4), :]
    u_ref[...] = mm(g_ref[...], y_ref[...])
    for slot in range(2):
        for s in range(2):

            @pl.when(info_ref[1 + slot] == s)
            def _():
                rows = lax.broadcasted_iota(jnp.int32, (n, 256), 0)
                cols = lax.broadcasted_iota(jnp.int32, (n, 256), 1)
                u_ref[:, slot * 256 : slot * 256 + 256] = jnp.where(rows == cols + s * 256, 1.0, 0.0).astype(
                    jnp.float32
                )

    solved = mm(g_ref[...], u_ref[...], 0, 0)
    at = 0
    for yh in range(4):
        for zlo in range(2):
            for half in range(2):
                for s in range(2):
                    row = s * 256 + (half * 8 + zlo * 4 + yh) * 16
                    o_ref[at : at + 16, :] = solved[row : row + 16, :]
                    at += 16


def solve(info, parts, factor):
    n = 512
    whole = pl.BlockSpec(memory_space=pltpu.VMEM)
    return pl.pallas_call(
        solve_kernel,
        out_shape=jax.ShapeDtypeStruct((n, n), jnp.float32),
        in_specs=[pl.BlockSpec(memory_space=pltpu.SMEM)] + [whole] * 5,
        out_specs=whole,
        scratch_shapes=[pltpu.VMEM((n, n), jnp.float32), pltpu.VMEM((n, n), jnp.float32)],
        cost_estimate=pl.CostEstimate(flops=4 * 6 * n**3, bytes_accessed=3 * 2**20, transcendentals=0),
    )(info, *parts, factor)


def update_kernel(info_ref, w_ref, own_ref, other_ref, z_ref, o_ref):
    step = pl.program_id(0)

    def rows_of(source, yl):
        for ch in range(2):
            panel = jnp.concatenate(
                [source[yh, yl, pl.ds(ch, 128, stride=2), :] for yh in range(4)], axis=0
            )
            change = mm(panel, z_ref[...], 0, 0)
            for j in range(4):
                hit = info_ref[1 + j // 2] >= 0
                keep = jnp.where(hit, 0.0, 1.0).astype(jnp.float32)
                sign = jnp.where(hit, 1.0, -1.0).astype(jnp.float32)
                at = pl.ds(ch * 512 + j, 128, stride=4)
                o_ref[at, :] = keep * w_ref[at, :] + sign * change[:, j * 128 : j * 128 + 128]

    for o, source in enumerate((own_ref, other_ref)):
        for yl in range(2):

            @pl.when(step == o * 2 + yl)
            def _():
                rows_of(source, yl)


def update(info, working, own, other, solved):
    n = 512
    whole = pl.BlockSpec(memory_space=pltpu.VMEM)

    def block(step, info_ref):
        core = info_ref[0]
        part = jnp.where(step >= 2, 1 - core, core)
        return (step % 2) * 2 + part, 0

    return pl.pallas_call(
        update_kernel,
        out_shape=jax.ShapeDtypeStruct(working.shape, jnp.float32),
        grid_spec=pltpu.PrefetchScalarGridSpec(
            num_scalar_prefetch=1,
            grid=(4,),
            in_specs=[pl.BlockSpec((1024, 128), block), whole, whole, whole],
            out_specs=pl.BlockSpec((1024, 128), block),
        ),
        cost_estimate=pl.CostEstimate(flops=4 * 6 * n**3, bytes_accessed=8 * 2**20, transcendentals=0),
    )(info, working, own, other, solved)


def swap(array, axis):
    return lax.ppermute(array, axis, [(0, 1), (1, 0)])


def ordered_pair(own, other, index):
    first = jnp.where(index == 0, own, other)
    second = jnp.where(index == 0, other, own)
    return jnp.stack([first, second])


def spread_pairs(swapped):
    pairs = []
    for source in range(512):
        blk, row = divmod(source, 16)
        upper = (row >= 8) != swapped
        target_row = blk // 4 + (8 if upper else 0)
        target_blk = (row % 8) * 4 + blk % 4
        pairs.append((source, target_blk * 16 + target_row))
    return pairs


EVERY = ("zlo", "y", "core", "x", "zhi")
ROWS = ("x", "zhi")


def pick(array, axis, index):
    return lax.dynamic_index_in_dim(array, index, axis, keepdims=False)


def exchange(array, axis):
    return lax.all_to_all(array, axis, 0, 0, tiled=True)


def copies(array, count):
    return jnp.broadcast_to(array, (count, *array.shape))


def doubled(array, axis):
    index = lax.axis_index(axis)
    near = lax.ppermute(array, axis, [(i, i ^ 1) for i in range(4)])
    pair = ordered_pair(array, near, index % 2)
    far = lax.ppermute(pair, axis, [(i, i ^ 2) for i in range(4)])
    return ordered_pair(pair, far, index // 2).reshape(4, *array.shape)


def after(array, *others):
    return lax.optimization_barrier((array, *others))[0]


def sections(covariance, panel_order):
    place = lax.axis_index(EVERY)
    row, core, zlo, blk = place & 15, (place >> 4) & 1, place >> 8, place >> 4
    working = covariance.reshape(4096, 128)
    target = [panel_order[0], panel_order[1]]
    root = [q >> 2 for q in target]

    cand = [lax.dynamic_slice_in_dim(working, (q & 3) << 10, 1024, 0).reshape(4, 4, 64, 128) for q in target]
    got = exchange(jnp.stack(cand, axis=2), "x")
    got = jnp.stack([pick(got[:, :, s], 0, root[s] >> 2) for s in range(2)], axis=1)
    hits = [jnp.int32(-1), jnp.int32(-1)]
    for i in range(2):
        for s in range(2):
            hits[i] = jnp.where(target[s] == i * 32 + blk, s, hits[i])
    info = jnp.stack([core, hits[0], hits[1], (place >> 2) & 3]).astype(jnp.int32)
    got = after(got, info)
    got = exchange(got, "zhi")
    chunk = jnp.stack([pick(got[:, s], 0, root[s] & 3) for s in range(2)])
    by_slot = chunk.reshape(2, 16, 2, 2, 128)

    part = [pick(by_slot[1 if i else 0], 1, target[1 if i == 2 else 0] >> 5) for i in range(3)]
    blocks = jnp.stack(part).reshape(3, 2, 16, 128)
    source = [target[0], target[0], target[1]]

    def chosen(shift, index, own, other):
        return jnp.stack([jnp.where(((source[i] >> shift) & 1) == index, own[i], other[i]) for i in range(3)])

    other = swap(pick(blocks, 1, 1 - core), "core")
    mine = chosen(0, core, pick(blocks, 1, core), other)
    other = swap(mine, "zlo")
    placed = mine = chosen(4, zlo, mine, other)
    spread = exchange(copies(mine, 8), "y")
    mine = jnp.stack([pick(spread[:, i], 0, (source[i] >> 1) & 7) for i in range(3)])
    mine = exchange(copies(mine, 4), "zhi")
    mine = exchange(copies(mine, 4), "x")
    other = swap(mine, "core")
    factor = inverse_factor(core.reshape(1), mine, other)

    across = doubled(chunk, "zhi")
    parts = [across]
    for shift in range(1, 4):
        parts.append(lax.ppermute(across, "x", [(i, (i + shift) % 4) for i in range(4)]))

    low, high = by_slot[:, :, 0].reshape(64, 128), by_slot[:, :, 1].reshape(64, 128)
    upper = row >= 8
    send_a = after(jnp.where(upper, high, low), placed)
    send_b = after(jnp.where(upper, low, high), placed)
    piece_a = lax.ppermute(send_a, EVERY, spread_pairs(False))
    piece_b = lax.ppermute(send_b, EVERY, spread_pairs(True))
    pieces = jnp.stack([jnp.where(upper, piece_b, piece_a), jnp.where(upper, piece_a, piece_b)])
    other = swap(pieces, "zlo")
    pieces = ordered_pair(pieces, other, zlo).reshape(256, 128)
    pieces = after(pieces, mine)
    pieces = exchange(copies(pieces, 8), "y").reshape(4, 2, 256, 128)
    other = swap(pieces, "core")

    solved = solve(info, parts, factor)
    result = update(info, working, pieces, other, solved)
    return result.reshape(1024, 2, 1, 256)


def solution(mesh):
    fine = Mesh(mesh.devices.reshape(2, 8, 2, 4, 4), EVERY)
    spec = P(ROWS, None, ("zlo", "y", "core"), None)
    return jax.shard_map(sections, mesh=fine, in_specs=(spec, P()), out_specs=spec, check_vma=False)
```
